32 devices in a mesh: grp: 2 (over x), feed: 16 (over z, y, core).
Axes of the slice: x: 2, y: 2, z: 4, core: 2. Of those that a mesh axis runs over, the one named last changes fastest.
Arguments:
- samples: bfloat16 [32, 256, 65536], P(('grp', 'feed')), parts along dimension 0, may hold values from -6 to 6
- pfb_taps: float32 [4, 8192], replicated, may hold values from -0.03125 to 0.03125
Outputs:
- visibility: float32 [16384, 4096], P(('grp', 'feed')), parts along dimension 0
The draws below stay inside these ranges and needn't reach their ends.
There are 2 independent parts, one for each index of `grp`. The reference program is written for one: setup_inputs(seed, part) draws one part's arguments, and reference() takes and returns one part's arrays. A program takes and returns all parts, laid end to end along the dimension named above; an argument that names none is the same for every part. Nothing has to cross between parts.
All inputs are finite; a program needn't handle non-finite values.
Results may differ from the reference program's by a relative error of at most 0.004.
Values may be sent and summed in bfloat16 or wider, within the bound.
A program may use at most 192 MiB of HBM per device.

```python
import math
import jax
import jax.numpy as jnp
from jax import lax

FEEDS = 2048
NFFT = 8192
TAPS = 4
FIRST_CH = 1536
TIME_BLOCKS = 2
FRAMES_DEV = 8
CH_SLAB = 4
NSPEC = 16
FEED_DEV = 256
N_FEED = 16


def block_levels(rng, dims, shards, least, largest):
    def one(dim, blocks):
        steps = jax.random.uniform(jax.random.fold_in(jax.random.fold_in(rng, 6), dim), (blocks,), jnp.float32, least / len(shards), largest / len(shards))
        return jnp.repeat(jnp.exp(steps), dims[dim] // blocks).reshape((-1,) + (1,) * (len(dims) - dim - 1))

    gain = one(*shards[0])
    for cut in shards[1:]:
        gain = gain * one(*cut)
    return gain


def bell_draw(own_key, dims, spread, bound, shards=(), held_as=jnp.bfloat16):
    entries = jax.random.normal(own_key, dims, jnp.float32) * spread
    if len(shards) > 0:
        entries = block_levels(own_key, dims, shards, -0.22, 0.18) * entries
    return jnp.clip(entries, min=-bound, max=bound).astype(held_as)


def setup_inputs(seed: int = 0, part: int = 0) -> dict:
    splits = jax.random.split(jax.random.key(seed), 3)
    own_keys = jax.random.split(jax.random.fold_in(splits[2], part), 3)
    return {
        "samples": bell_draw(own_keys[0], (N_FEED, FEED_DEV, FRAMES_DEV * NFFT), 1.0, 6.0, ((0, 16),)),
        "pfb_taps": bell_draw(splits[1], (TAPS, NFFT), (TAPS * NFFT) ** -0.5, 0.03125, (), jnp.float32),
    }


def dft_matrix(fft_len, first_channel, channel_count):
    sample_ids = jnp.arange(fft_len, dtype=jnp.int32)
    channel_ids = first_channel + jnp.arange(channel_count, dtype=jnp.int32)
    phase = (sample_ids[:, None] * channel_ids[None, :]) % fft_len
    angle = phase.astype(jnp.float32) * (2.0 * math.pi / fft_len)
    return jnp.concatenate([jnp.cos(angle), -jnp.sin(angle)], axis=1)


def reference(samples, pfb_taps):
    blocks = samples.reshape(TIME_BLOCKS, N_FEED // TIME_BLOCKS, FEED_DEV, FRAMES_DEV, NFFT)
    frames = jnp.transpose(blocks, (1, 2, 0, 3, 4)).reshape(FEEDS // FEED_DEV, FEED_DEV, NSPEC, NFFT)
    dft_table = dft_matrix(NFFT, FIRST_CH, CH_SLAB)

    def transform(part_frames):
        padded = jnp.concatenate([jnp.zeros((FEED_DEV, TAPS - 1, NFFT), part_frames.dtype), part_frames], axis=1)
        filtered = jnp.zeros((FEED_DEV, NSPEC, NFFT), jnp.float32)
        for tap_index in range(TAPS):
            filtered = filtered + padded[:, tap_index:tap_index + NSPEC].astype(jnp.float32) * pfb_taps[tap_index]
        spectra = jnp.dot(filtered.reshape(FEED_DEV * NSPEC, NFFT), dft_table, precision=lax.Precision.HIGHEST, preferred_element_type=jnp.float32)
        return spectra.astype(jnp.bfloat16).reshape(FEED_DEV, NSPEC, 2 * CH_SLAB)

    spectra = lax.map(transform, frames).reshape(FEEDS, NSPEC, 2 * CH_SLAB)
    real_all = jnp.moveaxis(spectra[:, :, :CH_SLAB], 2, 0)
    imag_all = jnp.moveaxis(spectra[:, :, CH_SLAB:], 2, 0)

    def correlate(pair):
        real_part, imag_part = pair
        all_feeds = jnp.concatenate([real_part, imag_part], axis=1)
        right_matrix = jnp.concatenate([all_feeds, jnp.concatenate([-imag_part, real_part], axis=1)], axis=0).T
        return jnp.dot(all_feeds, right_matrix, preferred_element_type=jnp.float32) * (1.0 / NSPEC)

    visibility = lax.map(correlate, (real_all, imag_all))
    return visibility.reshape(CH_SLAB * FEEDS, 2 * FEEDS)
```

```python
import functools
import math

import jax
import jax.numpy as jnp
import numpy as np
from jax import lax
from jax.experimental import pallas as pl
from jax.experimental.pallas import tpu as pltpu
from jax.sharding import PartitionSpec as P

FIRST_CH = 1536
TIME_BLOCKS = 2
ROWS_DEV = 512
TILE = 256
UNITS = 2
CHUNKS = 8
GROUPS = 2


def dft_rows(fft_len, channels):
    phase = (np.arange(fft_len)[None, :] * (FIRST_CH + np.arange(channels))[:, None]) % fft_len
    angle = phase * (2.0 * math.pi / fft_len)
    return np.concatenate([np.cos(angle), -np.sin(angle)], axis=0).astype(np.float32)


def channelize_kernel(
    devices, samples_ref, taps_ref, table_ref, out_ref,
    frames_buf, taps_buf, table_buf, w_buf, g_buf, spec_buf, msg_buf, spill_out, spill_in,
    load_sems, aux_sems, spill_sems, send_sem, recv_sem,
):
    me = lax.axis_index("feed")
    span = devices // TIME_BLOCKS
    frame_count, feeds, fft_len = frames_buf.shape
    tap_count = taps_buf.shape[0]
    cols = table_buf.shape[0]
    rows = tap_count * cols
    channels = cols // 2
    owners = devices // channels
    edge = tap_count - 1
    chunk = fft_len // CHUNKS
    early = frame_count - edge
    group_frames = frame_count // GROUPS

    aux = [
        pltpu.make_async_copy(taps_ref, taps_buf, aux_sems.at[0]),
        pltpu.make_async_copy(table_ref, table_buf, aux_sems.at[1]),
    ]
    for copy in aux:
        copy.start()

    def load(frame, part):
        start = pl.multiple_of(frame * fft_len + part * chunk, 128)
        here = pl.multiple_of(part * chunk, 128)
        return pltpu.make_async_copy(
            samples_ref.at[0, :, pl.ds(start, chunk)],
            frames_buf.at[frame, :, pl.ds(here, chunk)],
            load_sems.at[frame * CHUNKS + part],
        )

    def start_part(step, carry):
        group = GROUPS - 1 - step // CHUNKS
        for inner in range(group_frames):
            load(group * group_frames + inner, lax.rem(step, CHUNKS)).start()
        return carry

    lax.fori_loop(0, GROUPS * CHUNKS, start_part, 0)

    def wait_part(group, part):
        for inner in range(group_frames):
            load(group * group_frames + inner, part).wait()

    barrier = pltpu.get_barrier_semaphore()

    def greet(step, carry):
        peer = lax.rem(me + step, devices)
        pl.semaphore_signal(barrier, inc=1, device_id={"feed": peer}, device_id_type=pl.DeviceIdType.MESH)
        return carry

    lax.fori_loop(1, devices, greet, 0)

    for copy in aux:
        copy.wait()

    def build(part):
        for block in range(chunk // TILE):
            lines = pl.ds(pl.multiple_of(part * chunk + block * TILE, TILE), TILE)
            whole = jnp.concatenate(
                [taps_buf[tap : tap + 1, lines] * table_buf[:, lines] for tap in range(tap_count)], axis=0
            )
            upper = whole.astype(jnp.bfloat16)
            w_buf[:rows, lines] = upper
            w_buf[rows:, lines] = (whole - upper.astype(jnp.float32)).astype(jnp.bfloat16)

    build(0)

    def keep(frame, total):
        g_buf[frame] = total[:rows] + total[rows:]

    def end_first():
        pl.semaphore_wait(barrier, devices - 1)
        for later in range(edge):
            total = g_buf[early + later, 0:cols, :]
            for tap in range(1, edge - later):
                total = total + g_buf[early + later + tap, tap * cols : (tap + 1) * cols, :]
            spill_out[later] = total

        @pl.when(me < span)
        def _():
            spill.start()
            spill_in[...] = jnp.zeros_like(spill_in)

    spill = pltpu.make_async_remote_copy(
        src_ref=spill_out, dst_ref=spill_in, send_sem=spill_sems.at[0], recv_sem=spill_sems.at[1],
        device_id={"feed": lax.rem(me + span, devices)}, device_id_type=pl.DeviceIdType.MESH,
    )

    if feeds == TILE:
        per_unit = group_frames // UNITS
        order = [(block, inner) for block in range(chunk // TILE) for inner in range(per_unit)]

        def lines_of(part, block):
            return pl.ds(pl.multiple_of(part * chunk + block * TILE, TILE), TILE)

        def push(group, part, place):
            block, inner = order[place]
            for unit in range(UNITS):
                frame = group * group_frames + unit * per_unit + inner
                pltpu.matmul_push_rhs(
                    frames_buf[frame, :, lines_of(part, block)], place % 2, unit, transpose=True
                )

        def main(*totals):
            wait_part(GROUPS - 1, 0)
            push(GROUPS - 1, 0, 0)
            for group in reversed(range(GROUPS)):
                def do_part(part, carry, last=False):
                    if group == GROUPS - 1 and not last:
                        build(part + 1)
                    for place, (block, inner) in enumerate(order):
                        if place + 1 < len(order):
                            push(group, part, place + 1)
                        elif not last:
                            wait_part(group, part + 1)
                            push(group, part + 1, 0)
                        elif group > 0:
                            wait_part(group - 1, 0)
                            push(group - 1, 0, 0)
                        for unit in range(UNITS):
                            pltpu.matmul_acc_lhs(
                                totals[unit * per_unit + inner], w_buf[:, lines_of(part, block)],
                                load_staged_rhs=place % 2,
                            )
                    return carry

                lax.fori_loop(0, CHUNKS - 1, do_part, 0)
                do_part(CHUNKS - 1, 0, True)
                for index in range(group_frames):
                    keep(group * group_frames + index, pltpu.matmul_pop(totals[index]))
                if group == GROUPS - 1:
                    end_first()

        pl.run_scoped(
            main,
            *[pltpu.ACC(unit)((2 * rows, TILE), jnp.float32) for unit in range(UNITS) for _ in range(per_unit)],
        )
    else:
        for group in reversed(range(GROUPS)):
            total = None
            for part in range(CHUNKS):
                if group == GROUPS - 1 and part + 1 < CHUNKS:
                    build(part + 1)
                wait_part(group, part)
                lines = pl.ds(part * chunk, chunk)
                block = frames_buf[group * group_frames : (group + 1) * group_frames, :, lines]
                product = lax.dot_general(
                    w_buf[:, lines], block.reshape(group_frames * feeds, chunk), (((1,), (1,)), ((), ())),
                    preferred_element_type=jnp.float32,
                )
                total = product if total is None else total + product
            for inner in range(group_frames):
                keep(group * group_frames + inner, total[:, inner * feeds : (inner + 1) * feeds])
            if group == GROUPS - 1:
                end_first()

    @pl.when(me < span)
    def _():
        spill.wait_send()

    @pl.when(me >= span)
    def _():
        spill.wait_recv()

    for time in range(frame_count):
        total = spill_in[time] if time < edge else None
        for tap in range(tap_count):
            frame = time - edge + tap
            if frame >= 0:
                term = g_buf[frame, tap * cols : (tap + 1) * cols, :]
                total = term if total is None else total + term
        spec_buf[:, time, :] = total
    for channel in range(channels):
        msg_buf[channel] = jnp.concatenate(
            [spec_buf[channel], spec_buf[channels + channel]], axis=0
        ).astype(jnp.bfloat16)

    bits = [1 << place for place in range(devices.bit_length() - 1)]
    turns = [bit * (1 - 2 * lax.rem(me // bit, 2)) for bit in bits]
    for step in range(devices - 1, 0, -1):
        peer = me
        for bit, turn in zip(bits, turns):
            if step & bit:
                peer = peer + turn
        pltpu.make_async_remote_copy(
            src_ref=msg_buf.at[peer // owners], dst_ref=out_ref.at[me],
            send_sem=send_sem, recv_sem=recv_sem,
            device_id={"feed": peer}, device_id_type=pl.DeviceIdType.MESH,
        ).start()
    out_ref[me] = msg_buf[me // owners]
    others = out_ref.at[pl.ds(0, devices - 1)]
    pltpu.make_async_copy(others, others, recv_sem).wait()
    pltpu.make_async_copy(others, others, send_sem).wait()


def correlate_kernel(devices, gathered_ref, out_ref, right_buf):
    _, depth, feeds = gathered_ref.shape
    half = depth // 2
    span = devices // TIME_BLOCKS
    total_feeds = span * feeds
    owners = total_feeds // ROWS_DEV
    rows = out_ref.shape[0]
    me = lax.axis_index("feed")
    spectra_count = TIME_BLOCKS * half

    @pl.when(pl.program_id(0) == 0)
    def _():
        for block in range(TIME_BLOCKS):
            for group in range(span):
                right_buf[
                    block * depth : (block + 1) * depth, group * feeds : (group + 1) * feeds
                ] = gathered_ref[block * span + group]

    start = pl.multiple_of(lax.rem(me, owners) * ROWS_DEV + pl.program_id(0) * rows, 128)
    left = right_buf[:, pl.ds(start, rows)]
    wide = left.astype(jnp.float32)
    turned = []
    for block in range(TIME_BLOCKS):
        middle = block * depth + half
        turned += [wide[middle : middle + half], -wide[middle - half : middle]]
    both = jnp.concatenate([left, jnp.concatenate(turned, axis=0).astype(jnp.bfloat16)], axis=1)
    product = lax.dot_general(
        both, right_buf[...], (((0,), (0,)), ((), ())), preferred_element_type=jnp.float32
    ) * (1.0 / spectra_count)
    out_ref[:, :total_feeds] = product[:rows]
    out_ref[:, total_feeds:] = product[rows:]


def body(samples, pfb_taps):
    feeds = samples.shape[1]
    tap_count, fft_len = pfb_taps.shape
    frame_count = samples.shape[2] // fft_len
    devices = lax.axis_size("feed")
    total_feeds = feeds * (devices // TIME_BLOCKS)
    channels = devices * ROWS_DEV // total_feeds
    cols = 2 * channels
    edge = tap_count - 1
    table = jnp.asarray(dft_rows(fft_len, channels))
    anywhere = pl.BlockSpec(memory_space=pl.ANY)
    gathered = pl.pallas_call(
        functools.partial(channelize_kernel, devices),
        out_shape=pltpu.VMEM((devices, 2 * frame_count, feeds), jnp.bfloat16),
        in_specs=[anywhere] * 3,
        out_specs=pl.BlockSpec(memory_space=pltpu.VMEM),
        scratch_shapes=[
            pltpu.VMEM((frame_count, feeds, fft_len), jnp.bfloat16),
            pltpu.VMEM((tap_count, fft_len), jnp.float32),
            pltpu.VMEM((cols, fft_len), jnp.float32),
            pltpu.VMEM((2 * tap_count * cols, fft_len), jnp.bfloat16),
            pltpu.VMEM((frame_count, tap_count * cols, feeds), jnp.float32),
            pltpu.VMEM((cols, frame_count, feeds), jnp.float32),
            pltpu.VMEM((channels, 2 * frame_count, feeds), jnp.bfloat16),
            pltpu.VMEM((edge, cols, feeds), jnp.float32),
            pltpu.VMEM((edge, cols, feeds), jnp.float32),
            pltpu.SemaphoreType.DMA((frame_count * CHUNKS,)),
            pltpu.SemaphoreType.DMA((2,)),
            pltpu.SemaphoreType.DMA((2,)),
            pltpu.SemaphoreType.DMA,
            pltpu.SemaphoreType.DMA,
        ],
        compiler_params=pltpu.CompilerParams(
            collective_id=0, has_side_effects=True, vmem_limit_bytes=56 * 2**20
        ),
        name="channelize",
    )(samples, pfb_taps, table)
    block_rows = ROWS_DEV // 4
    return pl.pallas_call(
        functools.partial(correlate_kernel, devices),
        out_shape=jax.ShapeDtypeStruct((ROWS_DEV, 2 * total_feeds), jnp.float32),
        grid=(ROWS_DEV // block_rows,),
        in_specs=[pl.BlockSpec(gathered.shape, lambda i: (0, 0, 0))],
        out_specs=pl.BlockSpec((block_rows, 2 * total_feeds), lambda i: (i, 0)),
        scratch_shapes=[pltpu.VMEM((TIME_BLOCKS * 2 * frame_count, total_feeds), jnp.bfloat16)],
        compiler_params=pltpu.CompilerParams(vmem_limit_bytes=32 * 2**20),
        name="correlate",
    )(gathered)


def solution(mesh):
    placed = (P(("grp", "feed"), None, None), P())
    return jax.shard_map(
        body, mesh=mesh, in_specs=placed, out_specs=P(("grp", "feed"), None), check_vma=False
    )
```

```python
import functools
import math

import jax
import jax.numpy as jnp
import numpy as np
from jax import lax
from jax.experimental import pallas as pl
from jax.experimental.pallas import tpu as pltpu
from jax.sharding import PartitionSpec as P

FIRST_CH = 1536
TIME_BLOCKS = 2
ROWS_DEV = 512
TILE = 256
UNITS = 2
CHUNKS = 4
STREAMED = 2


def dft_rows(fft_len, channels):
    phase = (np.arange(fft_len)[None, :] * (FIRST_CH + np.arange(channels))[:, None]) % fft_len
    angle = phase * (2.0 * math.pi / fft_len)
    return np.concatenate([np.cos(angle), -np.sin(angle)], axis=0).astype(np.float32)


def channelize_kernel(
    devices, samples_ref, taps_ref, table_ref, out_ref,
    frames_buf, taps_buf, table_buf, w_buf, g_buf, spec_buf, msg_buf, spill_out, spill_in,
    load_sems, aux_sems, spill_sems, send_sem, recv_sem,
):
    me = lax.axis_index("feed")
    span = devices // TIME_BLOCKS
    frame_count, feeds, fft_len = frames_buf.shape
    tap_count = taps_buf.shape[0]
    cols = table_buf.shape[0]
    rows = tap_count * cols
    channels = cols // 2
    owners = devices // channels
    edge = tap_count - 1
    chunk = fft_len // CHUNKS
    early = frame_count - edge
    halves = ((early, frame_count), (0, early))

    aux = [
        pltpu.make_async_copy(taps_ref, taps_buf, aux_sems.at[0]),
        pltpu.make_async_copy(table_ref, table_buf, aux_sems.at[1]),
    ]
    for copy in aux:
        copy.start()

    def load(frame, part):
        start = pl.multiple_of(frame * fft_len + part * chunk, 128)
        here = pl.multiple_of(part * chunk, 128)
        return pltpu.make_async_copy(
            samples_ref.at[0, :, pl.ds(start, chunk)],
            frames_buf.at[frame, :, pl.ds(here, chunk)],
            load_sems.at[frame * CHUNKS + part],
        )

    for begin, end in halves:
        def start_part(part, carry):
            for frame in range(begin, end):
                load(frame, part).start()
            return carry

        lax.fori_loop(0, CHUNKS, start_part, 0)

    barrier = pltpu.get_barrier_semaphore()

    def greet(step, carry):
        peer = lax.rem(me + step, devices)
        pl.semaphore_signal(barrier, inc=1, device_id={"feed": peer}, device_id_type=pl.DeviceIdType.MESH)
        return carry

    lax.fori_loop(1, devices, greet, 0)

    for copy in aux:
        copy.wait()

    def build(part):
        for block in range(chunk // TILE):
            lines = pl.ds(pl.multiple_of(part * chunk + block * TILE, TILE), TILE)
            whole = jnp.concatenate(
                [taps_buf[tap : tap + 1, lines] * table_buf[:, lines] for tap in range(tap_count)], axis=0
            )
            upper = whole.astype(jnp.bfloat16)
            w_buf[:rows, lines] = upper
            w_buf[rows:, lines] = (whole - upper.astype(jnp.float32)).astype(jnp.bfloat16)

    build(0)

    def keep(frame, total):
        g_buf[frame] = total[:rows] + total[rows : 2 * rows]

    spill = pltpu.make_async_remote_copy(
        src_ref=spill_out, dst_ref=spill_in, send_sem=spill_sems.at[0], recv_sem=spill_sems.at[1],
        device_id={"feed": lax.rem(me + span, devices)}, device_id_type=pl.DeviceIdType.MESH,
    )

    def end_first():
        pl.semaphore_wait(barrier, devices - 1)
        for later in range(edge):
            total = g_buf[early + later, 0:cols, :]
            for tap in range(1, edge - later):
                total = total + g_buf[early + later + tap, tap * cols : (tap + 1) * cols, :]
            spill_out[later] = total

        @pl.when(me < span)
        def _():
            spill.start()
            spill_in[...] = jnp.zeros_like(spill_in)

    if feeds == TILE:
        steps = chunk // TILE // UNITS

        def lines_of(part, step, unit):
            return pl.ds(pl.multiple_of(part * chunk + (step * UNITS + unit) * TILE, TILE), TILE)

        def hold(frame, part, step, stage):
            for unit in range(UNITS):
                pltpu.matmul_push_rhs(frames_buf[frame, :, lines_of(part, step, unit)], stage, unit, transpose=True)

        def stream_weights(totals, part, step, stage):
            for unit in range(UNITS):
                pltpu.matmul_acc_lhs(totals[unit], w_buf[:, lines_of(part, step, unit)], load_staged_rhs=stage)

        def pop(totals):
            return functools.reduce(jnp.add, [pltpu.matmul_pop(total) for total in totals])

        def hold_weights(part, step):
            for unit in range(UNITS):
                lines = w_buf[:, lines_of(part, step, unit)]
                blank = jnp.zeros((TILE - 2 * rows, TILE), jnp.bfloat16)
                pltpu.matmul_push_rhs(jnp.concatenate([lines, blank], axis=0), 0, unit, transpose=True)

        def run_half(begin, end, building, *totals):
            middle = begin + STREAMED
            streamed = totals[:UNITS]
            held = [totals[UNITS * (index + 1) : UNITS * (index + 2)] for index in range(end - middle)]
            rest = [(frame, step) for frame in range(middle + 1, end) for step in range(steps)]

            def do_part(part, carry, last=False):
                for frame in range(begin, middle + 1):
                    load(frame, part).wait()
                if building and not last:
                    build(part + 1)
                for step in range(steps):
                    hold(middle, part, step, 1)
                    for unit in range(UNITS):
                        lines = lines_of(part, step, unit)
                        pltpu.matmul_acc_lhs(
                            streamed[unit], frames_buf[begin:middle, :, lines].reshape(STREAMED * feeds, TILE),
                            load_staged_rhs=0,
                        )
                    if step + 1 < steps:
                        hold_weights(part, step + 1)
                    elif rest:
                        load(rest[0][0], part).wait()
                        hold(rest[0][0], part, 0, 0)
                    elif not last:
                        hold_weights(part + 1, 0)
                    stream_weights(held[0], part, step, 1)
                if last:
                    both = pop(streamed)[:, :128]
                    for index in range(STREAMED):
                        keep(begin + index, both[index * feeds : (index + 1) * feeds].T)
                    keep(middle, pop(held[0]))
                for place, (frame, step) in enumerate(rest):
                    if place + 1 < len(rest):
                        coming, ahead = rest[place + 1]
                        if coming != frame:
                            load(coming, part).wait()
                        hold(coming, part, ahead, (place + 1) % 2)
                    elif not last:
                        hold_weights(part + 1, 0)
                    stream_weights(held[frame - middle], part, step, place % 2)
                    if last and step == steps - 1:
                        keep(frame, pop(held[frame - middle]))
                return carry

            hold_weights(0, 0)
            lax.fori_loop(0, CHUNKS - 1, do_part, 0)
            do_part(CHUNKS - 1, 0, True)

        def sums(height):
            return [pltpu.ACC(unit)((height, TILE), jnp.float32) for unit in range(UNITS)]

        for begin, end in halves:
            pl.run_scoped(
                functools.partial(run_half, begin, end, begin > 0),
                *sums(STREAMED * feeds), *(sums(2 * rows) * (end - begin - STREAMED)),
            )
            if begin > 0:
                end_first()
    else:
        for begin, end in halves:
            total = None
            for part in range(CHUNKS):
                if begin > 0 and part + 1 < CHUNKS:
                    build(part + 1)
                for frame in range(begin, end):
                    load(frame, part).wait()
                lines = pl.ds(part * chunk, chunk)
                product = lax.dot_general(
                    w_buf[:, lines], frames_buf[begin:end, :, lines].reshape((end - begin) * feeds, chunk),
                    (((1,), (1,)), ((), ())), preferred_element_type=jnp.float32,
                )
                total = product if total is None else total + product
            for frame in range(begin, end):
                keep(frame, total[:, (frame - begin) * feeds : (frame - begin + 1) * feeds])
            if begin > 0:
                end_first()

    @pl.when(me < span)
    def _():
        spill.wait_send()

    @pl.when(me >= span)
    def _():
        spill.wait_recv()

    for time in range(frame_count):
        total = spill_in[time] if time < edge else None
        for tap in range(tap_count):
            frame = time - edge + tap
            if frame >= 0:
                term = g_buf[frame, tap * cols : (tap + 1) * cols, :]
                total = term if total is None else total + term
        spec_buf[:, time, :] = total
    for channel in range(channels):
        msg_buf[channel] = jnp.concatenate(
            [spec_buf[channel], spec_buf[channels + channel]], axis=0
        ).astype(jnp.bfloat16)

    bits = [1 << place for place in range(devices.bit_length() - 1)]
    turns = [bit * (1 - 2 * lax.rem(me // bit, 2)) for bit in bits]
    for step in range(devices - 1, 0, -1):
        peer = me
        for bit, turn in zip(bits, turns):
            if step & bit:
                peer = peer + turn
        pltpu.make_async_remote_copy(
            src_ref=msg_buf.at[peer // owners], dst_ref=out_ref.at[me],
            send_sem=send_sem, recv_sem=recv_sem,
            device_id={"feed": peer}, device_id_type=pl.DeviceIdType.MESH,
        ).start()
    out_ref[me] = msg_buf[me // owners]
    others = out_ref.at[pl.ds(0, devices - 1)]
    pltpu.make_async_copy(others, others, recv_sem).wait()
    pltpu.make_async_copy(others, others, send_sem).wait()


def correlate_kernel(devices, gathered_ref, out_ref, right_buf):
    _, depth, feeds = gathered_ref.shape
    half = depth // 2
    span = devices // TIME_BLOCKS
    total_feeds = span * feeds
    owners = total_feeds // ROWS_DEV
    rows = out_ref.shape[0]
    me = lax.axis_index("feed")
    spectra_count = TIME_BLOCKS * half

    @pl.when(pl.program_id(0) == 0)
    def _():
        for block in range(TIME_BLOCKS):
            for group in range(span):
                right_buf[
                    block * depth : (block + 1) * depth, group * feeds : (group + 1) * feeds
                ] = gathered_ref[block * span + group]

    start = pl.multiple_of(lax.rem(me, owners) * ROWS_DEV + pl.program_id(0) * rows, 128)
    left = right_buf[:, pl.ds(start, rows)]
    wide = left.astype(jnp.float32)
    turned = []
    for block in range(TIME_BLOCKS):
        middle = block * depth + half
        turned += [wide[middle : middle + half], -wide[middle - half : middle]]
    both = jnp.concatenate([left, jnp.concatenate(turned, axis=0).astype(jnp.bfloat16)], axis=1)
    product = lax.dot_general(
        both, right_buf[...], (((0,), (0,)), ((), ())), preferred_element_type=jnp.float32
    ) * (1.0 / spectra_count)
    out_ref[:, :total_feeds] = product[:rows]
    out_ref[:, total_feeds:] = product[rows:]


def body(samples, pfb_taps):
    feeds = samples.shape[1]
    tap_count, fft_len = pfb_taps.shape
    frame_count = samples.shape[2] // fft_len
    devices = lax.axis_size("feed")
    total_feeds = feeds * (devices // TIME_BLOCKS)
    channels = devices * ROWS_DEV // total_feeds
    cols = 2 * channels
    edge = tap_count - 1
    table = jnp.asarray(dft_rows(fft_len, channels))
    anywhere = pl.BlockSpec(memory_space=pl.ANY)
    gathered = pl.pallas_call(
        functools.partial(channelize_kernel, devices),
        out_shape=pltpu.VMEM((devices, 2 * frame_count, feeds), jnp.bfloat16),
        in_specs=[anywhere] * 3,
        out_specs=pl.BlockSpec(memory_space=pltpu.VMEM),
        scratch_shapes=[
            pltpu.VMEM((frame_count, feeds, fft_len), jnp.bfloat16),
            pltpu.VMEM((tap_count, fft_len), jnp.float32),
            pltpu.VMEM((cols, fft_len), jnp.float32),
            pltpu.VMEM((2 * tap_count * cols, fft_len), jnp.bfloat16),
            pltpu.VMEM((frame_count, tap_count * cols, feeds), jnp.float32),
            pltpu.VMEM((cols, frame_count, feeds), jnp.float32),
            pltpu.VMEM((channels, 2 * frame_count, feeds), jnp.bfloat16),
            pltpu.VMEM((edge, cols, feeds), jnp.float32),
            pltpu.VMEM((edge, cols, feeds), jnp.float32),
            pltpu.SemaphoreType.DMA((frame_count * CHUNKS,)),
            pltpu.SemaphoreType.DMA((2,)),
            pltpu.SemaphoreType.DMA((2,)),
            pltpu.SemaphoreType.DMA,
            pltpu.SemaphoreType.DMA,
        ],
        compiler_params=pltpu.CompilerParams(
            collective_id=0, has_side_effects=True, vmem_limit_bytes=56 * 2**20
        ),
        name="channelize",
    )(samples, pfb_taps, table)
    block_rows = ROWS_DEV // 4
    return pl.pallas_call(
        functools.partial(correlate_kernel, devices),
        out_shape=jax.ShapeDtypeStruct((ROWS_DEV, 2 * total_feeds), jnp.float32),
        grid=(ROWS_DEV // block_rows,),
        in_specs=[pl.BlockSpec(gathered.shape, lambda i: (0, 0, 0))],
        out_specs=pl.BlockSpec((block_rows, 2 * total_feeds), lambda i: (i, 0)),
        scratch_shapes=[pltpu.VMEM((TIME_BLOCKS * 2 * frame_count, total_feeds), jnp.bfloat16)],
        compiler_params=pltpu.CompilerParams(vmem_limit_bytes=32 * 2**20),
        name="correlate",
    )(gathered)


def solution(mesh):
    placed = (P(("grp", "feed"), None, None), P())
    return jax.shard_map(
        body, mesh=mesh, in_specs=placed, out_specs=P(("grp", "feed"), None), check_vma=False
    )
```

```python
import functools
import math

import jax
import jax.numpy as jnp
import numpy as np
from jax import lax
from jax.experimental import pallas as pl
from jax.experimental.pallas import tpu as pltpu
from jax.sharding import PartitionSpec as P

FIRST_CH = 1536
TIME_BLOCKS = 2
ROWS_DEV = 512
COLUMNS = 256
TILE = 256
UNITS = 2
CHUNKS = 4
STREAMED = 2


def dft_rows(fft_len, channels):
    phase = (np.arange(fft_len)[None, :] * (FIRST_CH + np.arange(channels))[:, None]) % fft_len
    angle = phase * (2.0 * math.pi / fft_len)
    return np.concatenate([np.cos(angle), -np.sin(angle)], axis=0).astype(np.float32)


def channelize_kernel(
    devices, samples_ref, taps_ref, table_ref, out_ref,
    frames_buf, taps_buf, table_buf, w_buf, g_buf, spec_buf, msg_buf, spill_out, spill_in,
    load_sems, aux_sems, spill_sems, send_sem, recv_sem,
):
    me = lax.axis_index("feed")
    span = devices // TIME_BLOCKS
    frame_count, feeds, fft_len = frames_buf.shape
    tap_count = taps_buf.shape[0]
    cols = table_buf.shape[0]
    rows = tap_count * cols
    channels = cols // 2
    owners = devices // channels
    edge = tap_count - 1
    chunk = fft_len // CHUNKS
    early = frame_count - edge
    halves = ((early, frame_count), (0, early))

    aux = [
        pltpu.make_async_copy(taps_ref, taps_buf, aux_sems.at[0]),
        pltpu.make_async_copy(table_ref, table_buf, aux_sems.at[1]),
    ]
    for copy in aux:
        copy.start()

    def load(frame, part):
        start = pl.multiple_of(frame * fft_len + part * chunk, 128)
        here = pl.multiple_of(part * chunk, 128)
        return pltpu.make_async_copy(
            samples_ref.at[0, :, pl.ds(start, chunk)],
            frames_buf.at[frame, :, pl.ds(here, chunk)],
            load_sems.at[frame * CHUNKS + part],
        )

    for begin, end in halves:
        def start_part(part, carry):
            for frame in range(begin, end):
                load(frame, part).start()
            return carry

        lax.fori_loop(0, CHUNKS, start_part, 0)

    barrier = pltpu.get_barrier_semaphore()

    def greet(step, carry):
        peer = lax.rem(me + step, devices)
        pl.semaphore_signal(barrier, inc=1, device_id={"feed": peer}, device_id_type=pl.DeviceIdType.MESH)
        return carry

    lax.fori_loop(1, devices, greet, 0)

    for copy in aux:
        copy.wait()

    def build(part):
        for block in range(chunk // TILE):
            lines = pl.ds(pl.multiple_of(part * chunk + block * TILE, TILE), TILE)
            whole = jnp.concatenate(
                [taps_buf[tap : tap + 1, lines] * table_buf[:, lines] for tap in range(tap_count)], axis=0
            )
            upper = whole.astype(jnp.bfloat16)
            w_buf[:rows, lines] = upper
            w_buf[rows:, lines] = (whole - upper.astype(jnp.float32)).astype(jnp.bfloat16)

    build(0)

    def keep(frame, total):
        g_buf[frame] = total[:rows] + total[rows : 2 * rows]

    spill = pltpu.make_async_remote_copy(
        src_ref=spill_out, dst_ref=spill_in, send_sem=spill_sems.at[0], recv_sem=spill_sems.at[1],
        device_id={"feed": lax.rem(me + span, devices)}, device_id_type=pl.DeviceIdType.MESH,
    )

    def end_first():
        pl.semaphore_wait(barrier, devices - 1)
        for later in range(edge):
            total = g_buf[early + later, 0:cols, :]
            for tap in range(1, edge - later):
                total = total + g_buf[early + later + tap, tap * cols : (tap + 1) * cols, :]
            spill_out[later] = total

        @pl.when(me < span)
        def _():
            spill.start()
            spill_in[...] = jnp.zeros_like(spill_in)

    if feeds == TILE:
        steps = chunk // TILE // UNITS

        def lines_of(part, step, unit):
            return pl.ds(pl.multiple_of(part * chunk + (step * UNITS + unit) * TILE, TILE), TILE)

        def hold(frame, part, step, stage):
            for unit in range(UNITS):
                pltpu.matmul_push_rhs(frames_buf[frame, :, lines_of(part, step, unit)], stage, unit, transpose=True)

        def stream_weights(totals, part, step, stage):
            for unit in range(UNITS):
                pltpu.matmul_acc_lhs(totals[unit], w_buf[:, lines_of(part, step, unit)], load_staged_rhs=stage)

        def pop(totals):
            return functools.reduce(jnp.add, [pltpu.matmul_pop(total) for total in totals])

        def hold_weights(part, step):
            for unit in range(UNITS):
                lines = w_buf[:, lines_of(part, step, unit)]
                blank = jnp.zeros((TILE - 2 * rows, TILE), jnp.bfloat16)
                pltpu.matmul_push_rhs(jnp.concatenate([lines, blank], axis=0), 0, unit, transpose=True)

        def run_half(begin, end, building, *totals):
            middle = begin + STREAMED
            streamed = totals[:UNITS]
            held = [totals[UNITS * (index + 1) : UNITS * (index + 2)] for index in range(end - middle)]
            rest = [(frame, step) for frame in range(middle + 1, end) for step in range(steps)]

            def do_part(part, carry, last=False):
                for frame in range(begin, middle + 1):
                    load(frame, part).wait()
                if building and not last:
                    build(part + 1)
                for step in range(steps):
                    hold(middle, part, step, 1)
                    for unit in range(UNITS):
                        lines = lines_of(part, step, unit)
                        pltpu.matmul_acc_lhs(
                            streamed[unit], frames_buf[begin:middle, :, lines].reshape(STREAMED * feeds, TILE),
                            load_staged_rhs=0,
                        )
                    if step + 1 < steps:
                        hold_weights(part, step + 1)
                    elif rest:
                        load(rest[0][0], part).wait()
                        hold(rest[0][0], part, 0, 0)
                    elif not last:
                        hold_weights(part + 1, 0)
                    stream_weights(held[0], part, step, 1)
                if last:
                    both = pop(streamed)[:, :128]
                    for index in range(STREAMED):
                        keep(begin + index, both[index * feeds : (index + 1) * feeds].T)
                    keep(middle, pop(held[0]))
                for place, (frame, step) in enumerate(rest):
                    if place + 1 < len(rest):
                        coming, ahead = rest[place + 1]
                        if coming != frame:
                            load(coming, part).wait()
                        hold(coming, part, ahead, (place + 1) % 2)
                    elif not last:
                        hold_weights(part + 1, 0)
                    stream_weights(held[frame - middle], part, step, place % 2)
                    if last and step == steps - 1:
                        keep(frame, pop(held[frame - middle]))
                return carry

            hold_weights(0, 0)
            lax.fori_loop(0, CHUNKS - 1, do_part, 0)
            do_part(CHUNKS - 1, 0, True)

        def sums(height):
            return [pltpu.ACC(unit)((height, TILE), jnp.float32) for unit in range(UNITS)]

        for begin, end in halves:
            pl.run_scoped(
                functools.partial(run_half, begin, end, begin > 0),
                *sums(STREAMED * feeds), *(sums(2 * rows) * (end - begin - STREAMED)),
            )
            if begin > 0:
                end_first()
    else:
        for begin, end in halves:
            total = None
            for part in range(CHUNKS):
                if begin > 0 and part + 1 < CHUNKS:
                    build(part + 1)
                for frame in range(begin, end):
                    load(frame, part).wait()
                lines = pl.ds(part * chunk, chunk)
                product = lax.dot_general(
                    w_buf[:, lines], frames_buf[begin:end, :, lines].reshape((end - begin) * feeds, chunk),
                    (((1,), (1,)), ((), ())), preferred_element_type=jnp.float32,
                )
                total = product if total is None else total + product
            for frame in range(begin, end):
                keep(frame, total[:, (frame - begin) * feeds : (frame - begin + 1) * feeds])
            if begin > 0:
                end_first()

    @pl.when(me < span)
    def _():
        spill.wait_send()

    @pl.when(me >= span)
    def _():
        spill.wait_recv()

    for time in range(frame_count):
        total = spill_in[time] if time < edge else None
        for tap in range(tap_count):
            frame = time - edge + tap
            if frame >= 0:
                term = g_buf[frame, tap * cols : (tap + 1) * cols, :]
                total = term if total is None else total + term
        spec_buf[:, time, :] = total
    for channel in range(channels):
        msg_buf[channel] = jnp.concatenate(
            [spec_buf[channel], spec_buf[channels + channel]], axis=0
        ).astype(jnp.bfloat16)

    for step in range(devices - 1):
        peer = step + jnp.where(me <= step, 1, 0)
        pltpu.make_async_remote_copy(
            src_ref=msg_buf.at[peer // owners], dst_ref=out_ref.at[me],
            send_sem=send_sem, recv_sem=recv_sem,
            device_id={"feed": peer}, device_id_type=pl.DeviceIdType.MESH,
        ).start()
    out_ref[me] = msg_buf[me // owners]
    others = out_ref.at[pl.ds(0, devices - 1)]
    pltpu.make_async_copy(others, others, recv_sem).wait()
    pltpu.make_async_copy(others, others, send_sem).wait()


def correlate_kernel(devices, gathered_ref, out_ref, right_buf, left_buf, out_buf, store_sems):
    _, depth, feeds = gathered_ref.shape
    half = depth // 2
    span = devices // TIME_BLOCKS
    total_feeds = span * feeds
    owners = total_feeds // ROWS_DEV
    me = lax.axis_index("feed")
    spectra_count = TIME_BLOCKS * half

    for block in range(TIME_BLOCKS):
        for group in range(span):
            right_buf[
                block * depth : (block + 1) * depth, group * feeds : (group + 1) * feeds
            ] = gathered_ref[block * span + group]

    start = pl.multiple_of(lax.rem(me, owners) * ROWS_DEV, 128)
    wide = right_buf[:, pl.ds(start, ROWS_DEV)].astype(jnp.float32)
    turned = []
    for block in range(TIME_BLOCKS):
        middle = block * depth + half
        turned += [wide[middle : middle + half], -wide[middle - half : middle]]
    left_buf[:ROWS_DEV] = wide.T.astype(jnp.bfloat16)
    left_buf[ROWS_DEV:] = jnp.concatenate(turned, axis=0).T.astype(jnp.bfloat16)

    copies = []
    for place in range(total_feeds // COLUMNS):
        columns = pl.ds(place * COLUMNS, COLUMNS)
        product = jnp.dot(
            left_buf[...], right_buf[:, columns], preferred_element_type=jnp.float32
        ) * (1.0 / spectra_count)
        for part in range(2):
            out_buf[2 * place + part] = product[part * ROWS_DEV : (part + 1) * ROWS_DEV]
            copy = pltpu.make_async_copy(
                out_buf.at[2 * place + part],
                out_ref.at[:, pl.ds(part * total_feeds + place * COLUMNS, COLUMNS)],
                store_sems.at[2 * place + part],
            )
            copy.start()
            copies.append(copy)
    for copy in copies:
        copy.wait()


def body(samples, pfb_taps):
    feeds = samples.shape[1]
    tap_count, fft_len = pfb_taps.shape
    frame_count = samples.shape[2] // fft_len
    devices = lax.axis_size("feed")
    total_feeds = feeds * (devices // TIME_BLOCKS)
    channels = devices * ROWS_DEV // total_feeds
    cols = 2 * channels
    edge = tap_count - 1
    table = jnp.asarray(dft_rows(fft_len, channels))
    anywhere = pl.BlockSpec(memory_space=pl.ANY)
    gathered = pl.pallas_call(
        functools.partial(channelize_kernel, devices),
        out_shape=pltpu.VMEM((devices, 2 * frame_count, feeds), jnp.bfloat16),
        in_specs=[anywhere] * 3,
        out_specs=pl.BlockSpec(memory_space=pltpu.VMEM),
        scratch_shapes=[
            pltpu.VMEM((frame_count, feeds, fft_len), jnp.bfloat16),
            pltpu.VMEM((tap_count, fft_len), jnp.float32),
            pltpu.VMEM((cols, fft_len), jnp.float32),
            pltpu.VMEM((2 * tap_count * cols, fft_len), jnp.bfloat16),
            pltpu.VMEM((frame_count, tap_count * cols, feeds), jnp.float32),
            pltpu.VMEM((cols, frame_count, feeds), jnp.float32),
            pltpu.VMEM((channels, 2 * frame_count, feeds), jnp.bfloat16),
            pltpu.VMEM((edge, cols, feeds), jnp.float32),
            pltpu.VMEM((edge, cols, feeds), jnp.float32),
            pltpu.SemaphoreType.DMA((frame_count * CHUNKS,)),
            pltpu.SemaphoreType.DMA((2,)),
            pltpu.SemaphoreType.DMA((2,)),
            pltpu.SemaphoreType.DMA,
            pltpu.SemaphoreType.DMA,
        ],
        compiler_params=pltpu.CompilerParams(
            collective_id=0, has_side_effects=True, vmem_limit_bytes=56 * 2**20
        ),
        name="channelize",
    )(samples, pfb_taps, table)
    pieces = 2 * total_feeds // COLUMNS
    depth = TIME_BLOCKS * 2 * frame_count
    return pl.pallas_call(
        functools.partial(correlate_kernel, devices),
        out_shape=jax.ShapeDtypeStruct((ROWS_DEV, 2 * total_feeds), jnp.float32),
        in_specs=[pl.BlockSpec(memory_space=pltpu.VMEM)],
        out_specs=anywhere,
        scratch_shapes=[
            pltpu.VMEM((depth, total_feeds), jnp.bfloat16),
            pltpu.VMEM((2 * ROWS_DEV, depth), jnp.bfloat16),
            pltpu.VMEM((pieces, ROWS_DEV, COLUMNS), jnp.float32),
            pltpu.SemaphoreType.DMA((pieces,)),
        ],
        compiler_params=pltpu.CompilerParams(vmem_limit_bytes=32 * 2**20),
        name="correlate",
    )(gathered)


def solution(mesh):
    placed = (P(("grp", "feed"), None, None), P())
    return jax.shard_map(
        body, mesh=mesh, in_specs=placed, out_specs=P(("grp", "feed"), None), check_vma=False
    )
```

```python
import functools
import math

import jax
import jax.numpy as jnp
import numpy as np
from jax import lax
from jax.experimental import pallas as pl
from jax.experimental.pallas import tpu as pltpu
from jax.sharding import PartitionSpec as P

FIRST_CH = 1536
TIME_BLOCKS = 2
ROWS_DEV = 512
COLUMNS = 256
TILE = 256
UNITS = 2
CHUNKS = 4
STREAMED = 2


def dft_rows(fft_len, channels):
    phase = (np.arange(fft_len)[None, :] * (FIRST_CH + np.arange(channels))[:, None]) % fft_len
    angle = phase * (2.0 * math.pi / fft_len)
    return np.concatenate([np.cos(angle), -np.sin(angle)], axis=0).astype(np.float32)


def channelize_kernel(
    devices, samples_ref, taps_ref, table_ref, out_ref, left_ref, block_ref,
    side_buf, frames_buf, taps_buf, table_buf, w_buf, g_buf, spec_buf, msg_buf, spill_out, spill_in,
    load_sems, aux_sems, spill_sems, send_sem, recv_sems,
):
    me = lax.axis_index("feed")
    span = devices // TIME_BLOCKS
    frame_count, feeds, fft_len = frames_buf.shape
    tap_count = taps_buf.shape[0]
    cols = table_buf.shape[0]
    rows = tap_count * cols
    channels = cols // 2
    owners = devices // channels
    edge = tap_count - 1
    chunk = fft_len // CHUNKS
    early = frame_count - edge
    halves = ((early, frame_count), (0, early))

    aux = [
        pltpu.make_async_copy(taps_ref, taps_buf, aux_sems.at[0]),
        pltpu.make_async_copy(table_ref, table_buf, aux_sems.at[1]),
    ]
    for copy in aux:
        copy.start()

    def load(frame, part):
        start = pl.multiple_of(frame * fft_len + part * chunk, 128)
        here = pl.multiple_of(part * chunk, 128)
        return pltpu.make_async_copy(
            samples_ref.at[0, :, pl.ds(start, chunk)],
            frames_buf.at[frame, :, pl.ds(here, chunk)],
            load_sems.at[frame * CHUNKS + part],
        )

    for begin, end in halves:
        def start_part(part, carry):
            for frame in range(begin, end):
                load(frame, part).start()
            return carry

        lax.fori_loop(0, CHUNKS, start_part, 0)

    barrier = pltpu.get_barrier_semaphore()

    def greet(step, carry):
        peer = lax.rem(me + step, devices)
        pl.semaphore_signal(barrier, inc=1, device_id={"feed": peer}, device_id_type=pl.DeviceIdType.MESH)
        return carry

    lax.fori_loop(1, devices, greet, 0)

    for copy in aux:
        copy.wait()

    def build(part):
        for block in range(chunk // TILE):
            lines = pl.ds(pl.multiple_of(part * chunk + block * TILE, TILE), TILE)
            whole = jnp.concatenate(
                [taps_buf[tap : tap + 1, lines] * table_buf[:, lines] for tap in range(tap_count)], axis=0
            )
            upper = whole.astype(jnp.bfloat16)
            w_buf[:rows, lines] = upper
            w_buf[rows:, lines] = (whole - upper.astype(jnp.float32)).astype(jnp.bfloat16)

    build(0)

    def keep(frame, total):
        g_buf[frame] = total[:rows] + total[rows : 2 * rows]

    spill = pltpu.make_async_remote_copy(
        src_ref=spill_out, dst_ref=spill_in, send_sem=spill_sems.at[0], recv_sem=spill_sems.at[1],
        device_id={"feed": lax.rem(me + span, devices)}, device_id_type=pl.DeviceIdType.MESH,
    )

    def end_first():
        pl.semaphore_wait(barrier, devices - 1)
        for later in range(edge):
            total = g_buf[early + later, 0:cols, :]
            for tap in range(1, edge - later):
                total = total + g_buf[early + later + tap, tap * cols : (tap + 1) * cols, :]
            spill_out[later] = total

        @pl.when(me < span)
        def _():
            spill.start()
            spill_in[...] = jnp.zeros_like(spill_in)

    if feeds == TILE:
        steps = chunk // TILE // UNITS

        def lines_of(part, step, unit):
            return pl.ds(pl.multiple_of(part * chunk + (step * UNITS + unit) * TILE, TILE), TILE)

        def hold(frame, part, step, stage):
            for unit in range(UNITS):
                pltpu.matmul_push_rhs(frames_buf[frame, :, lines_of(part, step, unit)], stage, unit, transpose=True)

        def stream_weights(totals, part, step, stage):
            for unit in range(UNITS):
                pltpu.matmul_acc_lhs(totals[unit], w_buf[:, lines_of(part, step, unit)], load_staged_rhs=stage)

        def pop(totals):
            return functools.reduce(jnp.add, [pltpu.matmul_pop(total) for total in totals])

        def hold_weights(part, step):
            for unit in range(UNITS):
                lines = w_buf[:, lines_of(part, step, unit)]
                blank = jnp.zeros((TILE - 2 * rows, TILE), jnp.bfloat16)
                pltpu.matmul_push_rhs(jnp.concatenate([lines, blank], axis=0), 0, unit, transpose=True)

        def run_half(begin, end, building, *totals):
            middle = begin + STREAMED
            streamed = totals[:UNITS]
            held = [totals[UNITS * (index + 1) : UNITS * (index + 2)] for index in range(end - middle)]
            rest = [(frame, step) for frame in range(middle + 1, end) for step in range(steps)]

            def do_part(part, carry, last=False):
                for frame in range(begin, middle + 1):
                    load(frame, part).wait()
                if building and not last:
                    build(part + 1)
                for step in range(steps):
                    hold(middle, part, step, 1)
                    for unit in range(UNITS):
                        lines = lines_of(part, step, unit)
                        pltpu.matmul_acc_lhs(
                            streamed[unit], frames_buf[begin:middle, :, lines].reshape(STREAMED * feeds, TILE),
                            load_staged_rhs=0,
                        )
                    if step + 1 < steps:
                        hold_weights(part, step + 1)
                    elif rest:
                        load(rest[0][0], part).wait()
                        hold(rest[0][0], part, 0, 0)
                    elif not last:
                        hold_weights(part + 1, 0)
                    stream_weights(held[0], part, step, 1)
                if last:
                    both = pop(streamed)[:, :128]
                    for index in range(STREAMED):
                        keep(begin + index, both[index * feeds : (index + 1) * feeds].T)
                    keep(middle, pop(held[0]))
                for place, (frame, step) in enumerate(rest):
                    if place + 1 < len(rest):
                        coming, ahead = rest[place + 1]
                        if coming != frame:
                            load(coming, part).wait()
                        hold(coming, part, ahead, (place + 1) % 2)
                    elif not last:
                        hold_weights(part + 1, 0)
                    stream_weights(held[frame - middle], part, step, place % 2)
                    if last and step == steps - 1:
                        keep(frame, pop(held[frame - middle]))
                return carry

            hold_weights(0, 0)
            lax.fori_loop(0, CHUNKS - 1, do_part, 0)
            do_part(CHUNKS - 1, 0, True)

        def sums(height):
            return [pltpu.ACC(unit)((height, TILE), jnp.float32) for unit in range(UNITS)]

        for begin, end in halves:
            pl.run_scoped(
                functools.partial(run_half, begin, end, begin > 0),
                *sums(STREAMED * feeds), *(sums(2 * rows) * (end - begin - STREAMED)),
            )
            if begin > 0:
                end_first()
    else:
        for begin, end in halves:
            total = None
            for part in range(CHUNKS):
                if begin > 0 and part + 1 < CHUNKS:
                    build(part + 1)
                for frame in range(begin, end):
                    load(frame, part).wait()
                lines = pl.ds(part * chunk, chunk)
                product = lax.dot_general(
                    w_buf[:, lines], frames_buf[begin:end, :, lines].reshape((end - begin) * feeds, chunk),
                    (((1,), (1,)), ((), ())), preferred_element_type=jnp.float32,
                )
                total = product if total is None else total + product
            for frame in range(begin, end):
                keep(frame, total[:, (frame - begin) * feeds : (frame - begin + 1) * feeds])
            if begin > 0:
                end_first()

    @pl.when(me < span)
    def _():
        spill.wait_send()

    @pl.when(me >= span)
    def _():
        spill.wait_recv()

    for time in range(frame_count):
        total = spill_in[time] if time < edge else None
        for tap in range(tap_count):
            frame = time - edge + tap
            if frame >= 0:
                term = g_buf[frame, tap * cols : (tap + 1) * cols, :]
                total = term if total is None else total + term
        spec_buf[:, time, :] = total
    for channel in range(channels):
        msg_buf[channel] = jnp.concatenate(
            [spec_buf[channel], spec_buf[channels + channel]], axis=0
        ).astype(jnp.bfloat16)

    for step in range(devices - 1):
        peer = step + jnp.where(me <= step, 1, 0)
        pltpu.make_async_remote_copy(
            src_ref=msg_buf.at[peer // owners], dst_ref=out_ref.at[me],
            send_sem=send_sem, recv_sem=recv_sems.at[me],
            device_id={"feed": peer}, device_id_type=pl.DeviceIdType.MESH,
        ).start()
    out_ref[me] = msg_buf[me // owners]
    depth = 2 * frame_count
    taken = ROWS_DEV // feeds
    base = lax.rem(me, owners) * taken

    def arrive(source):
        @pl.when(source != me)
        def _():
            pltpu.make_async_copy(msg_buf.at[0], out_ref.at[source], recv_sems.at[source]).wait()

    for block in range(TIME_BLOCKS):
        for index in range(taken):
            source = block * span + base + index
            arrive(source)
            side_buf[block * depth : (block + 1) * depth, index * feeds : (index + 1) * feeds] = out_ref[source]
    wide = side_buf[...].astype(jnp.float32)
    turned = []
    for block in range(TIME_BLOCKS):
        middle = block * depth + frame_count
        turned += [wide[middle : middle + frame_count], -wide[middle - frame_count : middle]]
    sides = [wide, jnp.concatenate(turned, axis=0)]
    if feeds == TILE:

        def first_block(*totals):
            right = side_buf[:, :COLUMNS]
            blank = jnp.zeros((TILE - right.shape[0], TILE), jnp.bfloat16)
            fill = jnp.zeros((128 - right.shape[0], ROWS_DEV), jnp.float32)
            for part in range(2):
                pltpu.matmul_push_rhs(jnp.concatenate([right, blank], axis=0), 0, part)
                left = jnp.concatenate([sides[part], fill], axis=0).T.astype(jnp.bfloat16)
                left_ref[part * ROWS_DEV : (part + 1) * ROWS_DEV] = left[:, : right.shape[0]]
                wide_left = jnp.concatenate([left, jnp.zeros_like(left)], axis=1)
                pltpu.matmul_acc_lhs(totals[part], wide_left, load_staged_rhs=0)
            for part in range(2):
                block_ref[part] = pltpu.matmul_pop(totals[part]) * (1.0 / (TIME_BLOCKS * frame_count))

        pl.run_scoped(first_block, *[pltpu.ACC(part)((ROWS_DEV, COLUMNS), jnp.float32) for part in range(2)])
    else:
        for part in range(2):
            lines = pl.ds(part * ROWS_DEV, ROWS_DEV)
            left_ref[lines] = sides[part].T.astype(jnp.bfloat16)
            block_ref[part] = jnp.dot(
                left_ref[lines], side_buf[:, :COLUMNS], preferred_element_type=jnp.float32
            ) * (1.0 / (TIME_BLOCKS * frame_count))

    def arrive_later(index, carry):
        place = lax.rem(index, span - taken)
        block = index // (span - taken)
        arrive(block * span + lax.rem(base + taken + place, span))
        return carry

    lax.fori_loop(0, TIME_BLOCKS * (span - taken), arrive_later, 0)
    others = out_ref.at[pl.ds(0, devices - 1)]
    pltpu.make_async_copy(others, others, send_sem).wait()


def correlate_kernel(
    devices, gathered_ref, left_ref, block_ref, out_ref, right_buf, out_buf, store_sems
):
    _, depth, feeds = gathered_ref.shape
    span = devices // TIME_BLOCKS
    total_feeds = span * feeds
    owners = total_feeds // ROWS_DEV
    start = lax.rem(lax.axis_index("feed"), owners) * ROWS_DEV
    spectra_count = TIME_BLOCKS * (depth // 2)
    copies = []

    def send(source, place, part):
        first = part * total_feeds + lax.rem(start + place * COLUMNS, total_feeds)
        copy = pltpu.make_async_copy(
            source, out_ref.at[:, pl.ds(pl.multiple_of(first, COLUMNS), COLUMNS)], store_sems.at[2 * place + part]
        )
        copy.start()
        copies.append(copy)

    for part in range(2):
        send(block_ref.at[part], 0, part)
    for block in range(TIME_BLOCKS):
        for group in range(span):
            right_buf[
                block * depth : (block + 1) * depth, group * feeds : (group + 1) * feeds
            ] = gathered_ref[block * span + group]
    for place in range(1, total_feeds // COLUMNS):
        columns = pl.ds(pl.multiple_of(lax.rem(start + place * COLUMNS, total_feeds), COLUMNS), COLUMNS)
        product = jnp.dot(
            left_ref[...], right_buf[:, columns], preferred_element_type=jnp.float32
        ) * (1.0 / spectra_count)
        for part in range(2):
            out_buf[2 * place - 2 + part] = product[part * ROWS_DEV : (part + 1) * ROWS_DEV]
            send(out_buf.at[2 * place - 2 + part], place, part)
    for copy in copies:
        copy.wait()


def body(samples, pfb_taps):
    feeds = samples.shape[1]
    tap_count, fft_len = pfb_taps.shape
    frame_count = samples.shape[2] // fft_len
    devices = lax.axis_size("feed")
    total_feeds = feeds * (devices // TIME_BLOCKS)
    channels = devices * ROWS_DEV // total_feeds
    cols = 2 * channels
    edge = tap_count - 1
    table = jnp.asarray(dft_rows(fft_len, channels))
    anywhere = pl.BlockSpec(memory_space=pl.ANY)
    depth = TIME_BLOCKS * 2 * frame_count
    gathered, left, block = pl.pallas_call(
        functools.partial(channelize_kernel, devices),
        out_shape=(
            pltpu.VMEM((devices, 2 * frame_count, feeds), jnp.bfloat16),
            pltpu.VMEM((2 * ROWS_DEV, depth), jnp.bfloat16),
            pltpu.VMEM((2, ROWS_DEV, COLUMNS), jnp.float32),
        ),
        in_specs=[anywhere] * 3,
        out_specs=[pl.BlockSpec(memory_space=pltpu.VMEM)] * 3,
        scratch_shapes=[
            pltpu.VMEM((depth, ROWS_DEV), jnp.bfloat16),
            pltpu.VMEM((frame_count, feeds, fft_len), jnp.bfloat16),
            pltpu.VMEM((tap_count, fft_len), jnp.float32),
            pltpu.VMEM((cols, fft_len), jnp.float32),
            pltpu.VMEM((2 * tap_count * cols, fft_len), jnp.bfloat16),
            pltpu.VMEM((frame_count, tap_count * cols, feeds), jnp.float32),
            pltpu.VMEM((cols, frame_count, feeds), jnp.float32),
            pltpu.VMEM((channels, 2 * frame_count, feeds), jnp.bfloat16),
            pltpu.VMEM((edge, cols, feeds), jnp.float32),
            pltpu.VMEM((edge, cols, feeds), jnp.float32),
            pltpu.SemaphoreType.DMA((frame_count * CHUNKS,)),
            pltpu.SemaphoreType.DMA((2,)),
            pltpu.SemaphoreType.DMA((2,)),
            pltpu.SemaphoreType.DMA,
            pltpu.SemaphoreType.DMA((devices,)),
        ],
        compiler_params=pltpu.CompilerParams(
            collective_id=0, has_side_effects=True, vmem_limit_bytes=56 * 2**20
        ),
        name="channelize",
    )(samples, pfb_taps, table)
    pieces = 2 * total_feeds // COLUMNS
    return pl.pallas_call(
        functools.partial(correlate_kernel, devices),
        out_shape=jax.ShapeDtypeStruct((ROWS_DEV, 2 * total_feeds), jnp.float32),
        in_specs=[pl.BlockSpec(memory_space=pltpu.VMEM)] * 3,
        out_specs=anywhere,
        scratch_shapes=[
            pltpu.VMEM((depth, total_feeds), jnp.bfloat16),
            pltpu.VMEM((pieces - 2, ROWS_DEV, COLUMNS), jnp.float32),
            pltpu.SemaphoreType.DMA((pieces,)),
        ],
        compiler_params=pltpu.CompilerParams(vmem_limit_bytes=32 * 2**20),
        name="correlate",
    )(gathered, left, block)


def solution(mesh):
    placed = (P(("grp", "feed"), None, None), P())
    return jax.shard_map(
        body, mesh=mesh, in_specs=placed, out_specs=P(("grp", "feed"), None), check_vma=False
    )
```

```python
import functools
import math

import jax
import jax.numpy as jnp
import numpy as np
from jax import lax
from jax.experimental import pallas as pl
from jax.experimental.pallas import tpu as pltpu
from jax.sharding import PartitionSpec as P

FIRST_CH = 1536
TIME_BLOCKS = 2
ROWS_DEV = 512
COLUMNS = 256
TILE = 256
UNITS = 2
CHUNKS = 4
STREAMED = 2


def dft_rows(fft_len, channels):
    phase = (np.arange(fft_len)[None, :] * (FIRST_CH + np.arange(channels))[:, None]) % fft_len
    angle = phase * (2.0 * math.pi / fft_len)
    return np.concatenate([np.cos(angle), -np.sin(angle)], axis=0).astype(np.float32)


def channelize_kernel(
    devices, samples_ref, taps_ref, table_ref, out_ref, left_ref, block_ref,
    side_buf, frames_buf, taps_buf, table_buf, w_buf, g_buf, spec_buf, msg_buf, spill_out, spill_in,
    load_sems, aux_sems, spill_sems, send_sem, recv_sems,
):
    me = lax.axis_index("feed")
    span = devices // TIME_BLOCKS
    frame_count, feeds, fft_len = frames_buf.shape
    tap_count = taps_buf.shape[0]
    cols = table_buf.shape[0]
    rows = tap_count * cols
    channels = cols // 2
    owners = devices // channels
    edge = tap_count - 1
    chunk = fft_len // CHUNKS
    early = frame_count - edge
    halves = ((early, frame_count), (0, early))

    aux = [
        pltpu.make_async_copy(taps_ref, taps_buf, aux_sems.at[0]),
        pltpu.make_async_copy(table_ref, table_buf, aux_sems.at[1]),
    ]
    for copy in aux:
        copy.start()

    def load(frame, part):
        start = pl.multiple_of(frame * fft_len + part * chunk, 128)
        here = pl.multiple_of(part * chunk, 128)
        return pltpu.make_async_copy(
            samples_ref.at[0, :, pl.ds(start, chunk)],
            frames_buf.at[frame, :, pl.ds(here, chunk)],
            load_sems.at[frame * CHUNKS + part],
        )

    for begin, end in halves:
        def start_part(part, carry):
            for frame in range(begin, end):
                load(frame, part).start()
            return carry

        lax.fori_loop(0, CHUNKS, start_part, 0)

    barrier = pltpu.get_barrier_semaphore()

    def greet(step, carry):
        peer = lax.rem(me + step, devices)
        pl.semaphore_signal(barrier, inc=1, device_id={"feed": peer}, device_id_type=pl.DeviceIdType.MESH)
        return carry

    lax.fori_loop(1, devices, greet, 0)

    for copy in aux:
        copy.wait()

    def build_block(block, carry):
        lines = pl.ds(pl.multiple_of(block * TILE, TILE), TILE)
        whole = jnp.concatenate(
            [taps_buf[tap : tap + 1, lines] * table_buf[:, lines] for tap in range(tap_count)], axis=0
        )
        upper = whole.astype(jnp.bfloat16)
        w_buf[:rows, lines] = upper
        w_buf[rows:, lines] = (whole - upper.astype(jnp.float32)).astype(jnp.bfloat16)
        return carry

    def build(part):
        count = chunk // TILE
        lax.fori_loop(part * count, (part + 1) * count, build_block, 0)

    def keep(frame, total):
        g_buf[frame] = total[:rows] + total[rows : 2 * rows]

    spill = pltpu.make_async_remote_copy(
        src_ref=spill_out, dst_ref=spill_in, send_sem=spill_sems.at[0], recv_sem=spill_sems.at[1],
        device_id={"feed": lax.rem(me + span, devices)}, device_id_type=pl.DeviceIdType.MESH,
    )

    def end_first():
        pl.semaphore_wait(barrier, devices - 1)
        for later in range(edge):
            total = g_buf[early + later, 0:cols, :]
            for tap in range(1, edge - later):
                total = total + g_buf[early + later + tap, tap * cols : (tap + 1) * cols, :]
            spill_out[later] = total

        @pl.when(me < span)
        def _():
            spill.start()
            spill_in[...] = jnp.zeros_like(spill_in)

    if feeds == TILE:
        steps = chunk // TILE // UNITS

        def lines_of(part, step, unit):
            return pl.ds(pl.multiple_of(part * chunk + (step * UNITS + unit) * TILE, TILE), TILE)

        def hold(frame, part, step, stage):
            for unit in range(UNITS):
                pltpu.matmul_push_rhs(frames_buf[frame, :, lines_of(part, step, unit)], stage, unit, transpose=True)

        def stream_weights(totals, part, step, stage):
            for unit in range(UNITS):
                pltpu.matmul_acc_lhs(totals[unit], w_buf[:, lines_of(part, step, unit)], load_staged_rhs=stage)

        def pop(totals):
            return functools.reduce(jnp.add, [pltpu.matmul_pop(total) for total in totals])

        def hold_weights(part, step):
            for unit in range(UNITS):
                lines = w_buf[:, lines_of(part, step, unit)]
                blank = jnp.zeros((TILE - 2 * rows, TILE), jnp.bfloat16)
                pltpu.matmul_push_rhs(jnp.concatenate([lines, blank], axis=0), 0, unit, transpose=True)

        def run_half(begin, end, building, *totals):
            middle = begin + STREAMED
            streamed = totals[:UNITS]
            held = [totals[UNITS * (index + 1) : UNITS * (index + 2)] for index in range(end - middle)]
            rest = [(frame, step) for frame in range(middle + 1, end) for step in range(steps)]

            def do_part(part, carry, last=False):
                for frame in range(begin, middle + 1):
                    load(frame, part).wait()
                if building:
                    build(lax.rem(part + 1, CHUNKS))
                for step in range(steps):
                    hold(middle, part, step, 1)
                    for unit in range(UNITS):
                        lines = lines_of(part, step, unit)
                        pltpu.matmul_acc_lhs(
                            streamed[unit], frames_buf[begin:middle, :, lines].reshape(STREAMED * feeds, TILE),
                            load_staged_rhs=0,
                        )
                    if step + 1 < steps:
                        hold_weights(part, step + 1)
                    elif rest:
                        load(rest[0][0], part).wait()
                        hold(rest[0][0], part, 0, 0)
                    else:
                        hold_weights(lax.rem(part + 1, CHUNKS), 0)
                    stream_weights(held[0], part, step, 1)
                if last:
                    keep_early()
                for place, (frame, step) in enumerate(rest):
                    if place + 1 < len(rest):
                        coming, ahead = rest[place + 1]
                        if coming != frame:
                            load(coming, part).wait()
                        hold(coming, part, ahead, (place + 1) % 2)
                    elif not last:
                        hold_weights(part + 1, 0)
                    stream_weights(held[frame - middle], part, step, place % 2)
                    if last and step == steps - 1:
                        keep(frame, pop(held[frame - middle]))
                return carry

            def keep_early():
                both = pop(streamed)[:, :128]
                for index in range(STREAMED):
                    keep(begin + index, both[index * feeds : (index + 1) * feeds].T)
                keep(middle, pop(held[0]))

            if building:
                build(0)
                hold_weights(0, 0)
                lax.fori_loop(0, CHUNKS, do_part, 0)
                keep_early()
            else:
                lax.fori_loop(0, CHUNKS - 1, do_part, 0)
                do_part(CHUNKS - 1, 0, True)

        def sums(height):
            return [pltpu.ACC(unit)((height, TILE), jnp.float32) for unit in range(UNITS)]

        for begin, end in halves:
            pl.run_scoped(
                functools.partial(run_half, begin, end, begin > 0),
                *sums(STREAMED * feeds), *(sums(2 * rows) * (end - begin - STREAMED)),
            )
            if begin > 0:
                end_first()
    else:
        for begin, end in halves:
            total = None
            for part in range(CHUNKS):
                if begin > 0:
                    build(part)
                for frame in range(begin, end):
                    load(frame, part).wait()
                lines = pl.ds(part * chunk, chunk)
                product = lax.dot_general(
                    w_buf[:, lines], frames_buf[begin:end, :, lines].reshape((end - begin) * feeds, chunk),
                    (((1,), (1,)), ((), ())), preferred_element_type=jnp.float32,
                )
                total = product if total is None else total + product
            for frame in range(begin, end):
                keep(frame, total[:, (frame - begin) * feeds : (frame - begin + 1) * feeds])
            if begin > 0:
                end_first()

    @pl.when(me < span)
    def _():
        spill.wait_send()

    @pl.when(me >= span)
    def _():
        spill.wait_recv()

    for time in range(frame_count):
        total = spill_in[time] if time < edge else None
        for tap in range(tap_count):
            frame = time - edge + tap
            if frame >= 0:
                term = g_buf[frame, tap * cols : (tap + 1) * cols, :]
                total = term if total is None else total + term
        spec_buf[:, time, :] = total
    for channel in range(channels):
        msg_buf[channel] = jnp.concatenate(
            [spec_buf[channel], spec_buf[channels + channel]], axis=0
        ).astype(jnp.bfloat16)
        for index in range(owners):
            peer = channel * owners + index

            @pl.when(peer != me)
            def _():
                pltpu.make_async_remote_copy(
                    src_ref=msg_buf.at[channel], dst_ref=out_ref.at[me],
                    send_sem=send_sem, recv_sem=recv_sems.at[me],
                    device_id={"feed": peer}, device_id_type=pl.DeviceIdType.MESH,
                ).start()

    out_ref[me] = msg_buf[me // owners]
    depth = 2 * frame_count
    taken = ROWS_DEV // feeds
    base = lax.rem(me, owners) * taken

    def arrive(source):
        @pl.when(source != me)
        def _():
            pltpu.make_async_copy(msg_buf.at[0], out_ref.at[source], recv_sems.at[source]).wait()

    for block in range(TIME_BLOCKS):
        for index in range(taken):
            source = block * span + base + index
            arrive(source)
            side_buf[block * depth : (block + 1) * depth, index * feeds : (index + 1) * feeds] = out_ref[source]
    wide = side_buf[...].astype(jnp.float32)
    turned = []
    for block in range(TIME_BLOCKS):
        middle = block * depth + frame_count
        turned += [wide[middle : middle + frame_count], -wide[middle - frame_count : middle]]
    sides = [wide, jnp.concatenate(turned, axis=0)]
    if feeds == TILE:

        def first_block(*totals):
            right = side_buf[:, :COLUMNS]
            blank = jnp.zeros((TILE - right.shape[0], TILE), jnp.bfloat16)
            fill = jnp.zeros((128 - right.shape[0], ROWS_DEV), jnp.float32)
            for part in range(2):
                pltpu.matmul_push_rhs(jnp.concatenate([right, blank], axis=0), 0, part)
                left = jnp.concatenate([sides[part], fill], axis=0).T.astype(jnp.bfloat16)
                left_ref[part * ROWS_DEV : (part + 1) * ROWS_DEV] = left[:, : right.shape[0]]
                wide_left = jnp.concatenate([left, jnp.zeros_like(left)], axis=1)
                pltpu.matmul_acc_lhs(totals[part], wide_left, load_staged_rhs=0)
            for part in range(2):
                block_ref[part] = pltpu.matmul_pop(totals[part]) * (1.0 / (TIME_BLOCKS * frame_count))

        pl.run_scoped(first_block, *[pltpu.ACC(part)((ROWS_DEV, COLUMNS), jnp.float32) for part in range(2)])
    else:
        for part in range(2):
            lines = pl.ds(part * ROWS_DEV, ROWS_DEV)
            left_ref[lines] = sides[part].T.astype(jnp.bfloat16)
            block_ref[part] = jnp.dot(
                left_ref[lines], side_buf[:, :COLUMNS], preferred_element_type=jnp.float32
            ) * (1.0 / (TIME_BLOCKS * frame_count))

    def arrive_later(index, carry):
        place = lax.rem(index, span - taken)
        block = index // (span - taken)
        arrive(block * span + lax.rem(base + taken + place, span))
        return carry

    lax.fori_loop(0, TIME_BLOCKS * (span - taken), arrive_later, 0)
    others = out_ref.at[pl.ds(0, devices - 1)]
    pltpu.make_async_copy(others, others, send_sem).wait()


def correlate_kernel(
    devices, gathered_ref, left_ref, block_ref, out_ref, right_buf, out_buf, store_sems
):
    _, depth, feeds = gathered_ref.shape
    span = devices // TIME_BLOCKS
    total_feeds = span * feeds
    owners = total_feeds // ROWS_DEV
    start = lax.rem(lax.axis_index("feed"), owners) * ROWS_DEV
    spectra_count = TIME_BLOCKS * (depth // 2)
    copies = []

    def send(source, place, part):
        first = part * total_feeds + lax.rem(start + place * COLUMNS, total_feeds)
        copy = pltpu.make_async_copy(
            source, out_ref.at[:, pl.ds(pl.multiple_of(first, COLUMNS), COLUMNS)], store_sems.at[2 * place + part]
        )
        copy.start()
        copies.append(copy)

    for part in range(2):
        send(block_ref.at[part], 0, part)
    for block in range(TIME_BLOCKS):
        for group in range(span):
            right_buf[
                block * depth : (block + 1) * depth, group * feeds : (group + 1) * feeds
            ] = gathered_ref[block * span + group]
    for place in range(1, total_feeds // COLUMNS):
        columns = pl.ds(pl.multiple_of(lax.rem(start + place * COLUMNS, total_feeds), COLUMNS), COLUMNS)
        product = jnp.dot(
            left_ref[...], right_buf[:, columns], preferred_element_type=jnp.float32
        ) * (1.0 / spectra_count)
        for part in range(2):
            out_buf[2 * place - 2 + part] = product[part * ROWS_DEV : (part + 1) * ROWS_DEV]
            send(out_buf.at[2 * place - 2 + part], place, part)
    for copy in copies:
        copy.wait()


def body(samples, pfb_taps):
    feeds = samples.shape[1]
    tap_count, fft_len = pfb_taps.shape
    frame_count = samples.shape[2] // fft_len
    devices = lax.axis_size("feed")
    total_feeds = feeds * (devices // TIME_BLOCKS)
    channels = devices * ROWS_DEV // total_feeds
    cols = 2 * channels
    edge = tap_count - 1
    table = jnp.asarray(dft_rows(fft_len, channels))
    anywhere = pl.BlockSpec(memory_space=pl.ANY)
    depth = TIME_BLOCKS * 2 * frame_count
    gathered, left, block = pl.pallas_call(
        functools.partial(channelize_kernel, devices),
        out_shape=(
            pltpu.VMEM((devices, 2 * frame_count, feeds), jnp.bfloat16),
            pltpu.VMEM((2 * ROWS_DEV, depth), jnp.bfloat16),
            pltpu.VMEM((2, ROWS_DEV, COLUMNS), jnp.float32),
        ),
        in_specs=[anywhere] * 3,
        out_specs=[pl.BlockSpec(memory_space=pltpu.VMEM)] * 3,
        scratch_shapes=[
            pltpu.VMEM((depth, ROWS_DEV), jnp.bfloat16),
            pltpu.VMEM((frame_count, feeds, fft_len), jnp.bfloat16),
            pltpu.VMEM((tap_count, fft_len), jnp.float32),
            pltpu.VMEM((cols, fft_len), jnp.float32),
            pltpu.VMEM((2 * tap_count * cols, fft_len), jnp.bfloat16),
            pltpu.VMEM((frame_count, tap_count * cols, feeds), jnp.float32),
            pltpu.VMEM((cols, frame_count, feeds), jnp.float32),
            pltpu.VMEM((channels, 2 * frame_count, feeds), jnp.bfloat16),
            pltpu.VMEM((edge, cols, feeds), jnp.float32),
            pltpu.VMEM((edge, cols, feeds), jnp.float32),
            pltpu.SemaphoreType.DMA((frame_count * CHUNKS,)),
            pltpu.SemaphoreType.DMA((2,)),
            pltpu.SemaphoreType.DMA((2,)),
            pltpu.SemaphoreType.DMA,
            pltpu.SemaphoreType.DMA((devices,)),
        ],
        compiler_params=pltpu.CompilerParams(
            collective_id=0, has_side_effects=True, vmem_limit_bytes=56 * 2**20
        ),
        name="channelize",
    )(samples, pfb_taps, table)
    pieces = 2 * total_feeds // COLUMNS
    return pl.pallas_call(
        functools.partial(correlate_kernel, devices),
        out_shape=jax.ShapeDtypeStruct((ROWS_DEV, 2 * total_feeds), jnp.float32),
        in_specs=[pl.BlockSpec(memory_space=pltpu.VMEM)] * 3,
        out_specs=anywhere,
        scratch_shapes=[
            pltpu.VMEM((depth, total_feeds), jnp.bfloat16),
            pltpu.VMEM((pieces - 2, ROWS_DEV, COLUMNS), jnp.float32),
            pltpu.SemaphoreType.DMA((pieces,)),
        ],
        compiler_params=pltpu.CompilerParams(vmem_limit_bytes=32 * 2**20),
        name="correlate",
    )(gathered, left, block)


def solution(mesh):
    placed = (P(("grp", "feed"), None, None), P())
    return jax.shard_map(
        body, mesh=mesh, in_specs=placed, out_specs=P(("grp", "feed"), None), check_vma=False
    )
```
